32 devices in a mesh: ctx: 16 (over z, x, core), tp: 2 (over y).
Axes of the slice: x: 2, y: 2, z: 4, core: 2. Of those that a mesh axis runs over, the one named last changes fastest.
Arguments:
- query_raw: bfloat16 [6144, 32, 128], P('ctx', 'tp'), may hold values from -12 to 12
- key_raw: bfloat16 [6144, 16, 128], P('ctx', 'tp'), may hold values from -12 to 12
- values: bfloat16 [6144, 16, 128], P('ctx', 'tp'), may hold values from -6 to 6
- query_gain: float32 [128], replicated, may hold values from 0.1 to 6
- key_gain: float32 [128], replicated, may hold values from 0.1 to 6
- documents: int32 [6144], replicated, may hold values from 0 to 3, never falling along the last dimension, each value on 1 to 3072 neighbouring positions
- upstream: bfloat16 [6144, 32, 128], P('ctx', 'tp'), may hold values from -6 to 6
Outputs:
- query_grad: bfloat16 [6144, 32, 128], P('ctx', 'tp')
- key_grad: bfloat16 [6144, 16, 128], P('ctx', 'tp')
- value_grad: bfloat16 [6144, 16, 128], P('ctx', 'tp')
- query_gain_grad: float32 [128], replicated
- key_gain_grad: float32 [128], replicated
The draws below stay inside these ranges and needn't reach their ends.
Inputs may be any that keep to these rules, and one draw needn't show every extreme that they name: `documents`: document ids never fall along the tokens; every id from 0 to 3 occurs, each on 1 to 3072 tokens, and one document has exactly 3072 tokens.
All inputs are finite; a program needn't handle non-finite values.
Results may differ from the reference program's by a relative error of at most 0.035.
Values may be sent and summed in bfloat16 or wider, within the bound.
A program may use at most 192 MiB of HBM per device.

```python
import math
import jax
import jax.numpy as jnp
import numpy as np
from jax import lax

QUERY_HEADS = 32
KEY_VALUE_HEADS = 16
HEAD_WIDTH = 128
QUERY_SCALAR = 168
TOK_DEV = 384
REACH = 8
PACKED_TOKENS = 6144
MOST = 3072
DOCS = 4


def gain_pair(key):
    first_key = jax.random.fold_in(key, 101)
    second_key = jax.random.fold_in(key, 202)
    query_side = 1.0 + 0.18 * jnp.clip(jax.random.normal(first_key, (HEAD_WIDTH,), jnp.float32), -5.0, 5.0)
    key_side = 1.0 + 0.18 * jnp.clip(jax.random.normal(second_key, (HEAD_WIDTH,), jnp.float32), -5.0, 5.0)
    return (query_side, key_side)


def draw_query_gain(key, part):
    return gain_pair(key)[0]


def draw_key_gain(key, part):
    return gain_pair(key)[1]


def draw_query_raw(key, part):
    key_matrix = jax.random.fold_in(key, 404)
    return jnp.clip(jax.random.normal(key_matrix, (PACKED_TOKENS, QUERY_HEADS, HEAD_WIDTH), jnp.float32), -6.0, 6.0).astype(jnp.bfloat16)


def draw_key_raw(key, part):
    key_matrix = jax.random.fold_in(key, 505)
    return jnp.clip(jax.random.normal(key_matrix, (PACKED_TOKENS, KEY_VALUE_HEADS, HEAD_WIDTH), jnp.float32), -6.0, 6.0).astype(jnp.bfloat16)


def steps_of(rng, extent, split, low, largest):
    loudness, own = 1.0, jax.random.fold_in(rng, 6)
    for axis_at, parts in split:
        heights = jnp.exp(jax.random.uniform(jax.random.fold_in(own, axis_at), (parts,), jnp.float32, low / len(split), largest / len(split)))
        loudness = loudness * jnp.repeat(heights, extent[axis_at] // parts).reshape([-1 if axis == axis_at else 1 for axis in range(len(extent))])
    return loudness


def profile(number_of, total, bound, slope):
    portions = [(1 << 20) // math.isqrt(standing ** slope) + 1 for standing in range(2, number_of + 1)]
    rest, given = total - bound - (number_of - 1), [1] * (number_of - 1)
    while rest > 0:
        free = [i for i in range(number_of - 1) if given[i] < bound]
        mass, remaining = sum([portions[i] for i in free]), rest
        for i in free:
            more = min(bound - given[i], max(1, remaining * portions[i] // mass), rest)
            given[i] = given[i] + more
            rest = rest - more
    return np.array([bound] + given)


def ragged_sizes(rng, count, total, reach, skew):
    if count == 2:
        one = jax.random.randint(rng, (), max(1, total - reach), min(reach, total - 1) + 1)
        return jnp.stack([one, total - one])
    tallies = jnp.asarray(profile(count, total, reach, skew), jnp.int32)
    pairs = (count - 1) // 2
    source_of, sink = tallies[1:1 + 2 * pairs:2], tallies[2:2 + 2 * pairs:2]
    slack = jnp.minimum(source_of - 1, reach - sink)
    shifted = jax.random.randint(jax.random.fold_in(rng, 1), (pairs,), 0, 1 << 20) % (slack + 1)
    tallies = tallies.at[1:1 + 2 * pairs:2].set(source_of - shifted).at[2:2 + 2 * pairs:2].set(sink + shifted)
    return tallies[jax.random.permutation(jax.random.fold_in(rng, 2), count)]


def scatter_about(own_key, extent, scale, most, cuts=(), held_as=jnp.bfloat16):
    drawn = scale * jax.random.normal(own_key, extent, jnp.float32)
    if cuts:
        drawn = drawn * steps_of(own_key, extent, cuts, -0.22, 0.18)
    return jnp.clip(drawn, -most, most).astype(held_as)


def setup_inputs(seed: int = 0) -> dict:
    keys = jax.random.split(jax.random.key(seed), 8)
    query_raw = draw_query_raw(jax.random.fold_in(keys[7], 71), 0)
    key_raw = draw_key_raw(jax.random.fold_in(keys[7], 71), 0)
    values = scatter_about(keys[2], (PACKED_TOKENS, KEY_VALUE_HEADS, HEAD_WIDTH), 1.0, 6.0, ((0, 16), (1, 2)))
    query_gain = draw_query_gain(jax.random.fold_in(keys[7], 71), 0)
    key_gain = draw_key_gain(jax.random.fold_in(keys[7], 71), 0)
    documents = jnp.searchsorted(jnp.cumsum(ragged_sizes(keys[5], DOCS, PACKED_TOKENS, MOST, 2)), jnp.arange(PACKED_TOKENS), side="right").astype(jnp.int32)
    upstream = scatter_about(keys[6], (PACKED_TOKENS, QUERY_HEADS, HEAD_WIDTH), 1.0, 6.0, ((0, 16), (1, 2)))
    return dict(query_raw=query_raw, key_raw=key_raw, values=values, query_gain=query_gain, key_gain=key_gain, documents=documents, upstream=upstream)


rope_base = 1000000.0
norm_eps = 1e-06

def rotate(inputs, gain_vec, positions):
    meansq = lax.optimization_barrier(jnp.mean(inputs * inputs, axis=-1, keepdims=True))
    normed = inputs * lax.rsqrt(meansq + norm_eps) * gain_vec
    half_dim = inputs.shape[-1] // 2
    inverse_freq = rope_base ** (-2.0 * jnp.arange(half_dim, dtype=jnp.float32) / inputs.shape[-1])
    angles = positions.astype(jnp.float32)[:, None] * inverse_freq[None, :]
    cosine = jnp.cos(angles)[:, None, :]
    sine_part = jnp.sin(angles)[:, None, :]
    leading = normed[..., :half_dim]
    trailing = normed[..., half_dim:]
    return jnp.concatenate([leading * cosine - trailing * sine_part, trailing * cosine + leading * sine_part], axis=-1)

def reference(query_raw, key_raw, values, query_gain, key_gain, documents, upstream):
    factor = QUERY_SCALAR ** (-0.5)
    head_grouping = QUERY_HEADS // KEY_VALUE_HEADS
    positions = jnp.arange(PACKED_TOKENS, dtype=jnp.int32)
    query_in = query_raw.astype(jnp.float32)
    key_in = key_raw.astype(jnp.float32)
    query_turned = rotate(query_in, query_gain, positions)
    key_rot = rotate(key_in, key_gain, positions)
    query_half_precision = lax.optimization_barrier(query_turned.astype(jnp.bfloat16)).reshape(PACKED_TOKENS, KEY_VALUE_HEADS, head_grouping, HEAD_WIDTH)
    key_half_precision = lax.optimization_barrier(key_rot.astype(jnp.bfloat16))
    incoming_gradient_groups = upstream.reshape(PACKED_TOKENS, KEY_VALUE_HEADS, head_grouping, HEAD_WIDTH)
    error_tolerance = REACH * TOK_DEV
    key_span = error_tolerance + TOK_DEV
    key_padded = jnp.concatenate([jnp.zeros((error_tolerance, KEY_VALUE_HEADS, HEAD_WIDTH), jnp.bfloat16), key_half_precision], axis=0)
    value_padded = jnp.concatenate([jnp.zeros((error_tolerance, KEY_VALUE_HEADS, HEAD_WIDTH), jnp.bfloat16), values], axis=0)
    doc_pad = jnp.concatenate([jnp.full((error_tolerance,), -1, jnp.int32), documents.astype(jnp.int32)], axis=0)
    pos_pad = jnp.arange(PACKED_TOKENS + error_tolerance, dtype=jnp.int32) - error_tolerance

    def one_block(accums, block_num):
        key_acc, value_acc = accums
        row_start = (block_num * TOK_DEV).astype(jnp.int32)
        query_blk = lax.dynamic_slice_in_dim(query_half_precision, row_start, TOK_DEV, 0).astype(jnp.float32)
        upstream_blk = lax.dynamic_slice_in_dim(incoming_gradient_groups, row_start, TOK_DEV, 0).astype(jnp.float32)
        query_docs = lax.dynamic_slice_in_dim(documents.astype(jnp.int32), row_start, TOK_DEV, 0)
        query_pos = row_start + jnp.arange(TOK_DEV, dtype=jnp.int32)
        key_blk = lax.dynamic_slice_in_dim(key_padded, row_start, key_span, 0).astype(jnp.float32)
        value_blk = lax.dynamic_slice_in_dim(value_padded, row_start, key_span, 0).astype(jnp.float32)
        key_docs = lax.dynamic_slice_in_dim(doc_pad, row_start, key_span, 0)
        key_pos = lax.dynamic_slice_in_dim(pos_pad, row_start, key_span, 0)
        visible = (query_docs[:, None] == key_docs[None, :]) & (key_pos[None, :] <= query_pos[:, None])
        scores = jnp.where(visible[None, None], factor * jnp.einsum('igrd,jgd->grij', query_blk, key_blk), -1e+30)
        row_peak = lax.optimization_barrier(jnp.max(scores, axis=-1))
        log_norm = row_peak + jnp.log(lax.optimization_barrier(jnp.sum(jnp.exp(scores - row_peak[..., None]), axis=-1)))
        attend = jnp.where(visible[None, None], jnp.exp(scores - log_norm[..., None]), 0.0)
        attend_bf = lax.optimization_barrier(attend.astype(jnp.bfloat16)).astype(jnp.float32)
        attend_grad = jnp.einsum('igrd,jgd->grij', upstream_blk, value_blk)
        row_delta = lax.optimization_barrier(jnp.sum(attend_bf * attend_grad, axis=-1))
        score_grad = lax.optimization_barrier((attend * (attend_grad - row_delta[..., None])).astype(jnp.bfloat16)).astype(jnp.float32)
        query_part = factor * jnp.einsum('grij,jgd->igrd', score_grad, key_blk)
        key_part = factor * jnp.einsum('grij,igrd->jgd', score_grad, query_blk)
        value_part = jnp.einsum('grij,igrd->jgd', attend_bf, upstream_blk)
        key_acc = lax.dynamic_update_slice_in_dim(key_acc, lax.dynamic_slice_in_dim(key_acc, row_start, key_span, 0) + key_part, row_start, 0)
        value_acc = lax.dynamic_update_slice_in_dim(value_acc, lax.dynamic_slice_in_dim(value_acc, row_start, key_span, 0) + value_part, row_start, 0)
        return ((key_acc, value_acc), query_part)
    initial_accumulators = (jnp.zeros((PACKED_TOKENS + error_tolerance, KEY_VALUE_HEADS, HEAD_WIDTH), jnp.float32), jnp.zeros((PACKED_TOKENS + error_tolerance, KEY_VALUE_HEADS, HEAD_WIDTH), jnp.float32))
    (key_acc, value_acc), query_parts = lax.scan(one_block, initial_accumulators, jnp.arange(PACKED_TOKENS // TOK_DEV, dtype=jnp.int32))
    query_rot_grad = query_parts.reshape(PACKED_TOKENS, QUERY_HEADS, HEAD_WIDTH)
    key_rot_grad = key_acc[error_tolerance:]
    value_grad = value_acc[error_tolerance:].astype(jnp.bfloat16)
    unused_query, query_pull = jax.vjp(lambda inputs, gain_vec: rotate(inputs, gain_vec, positions), query_in, query_gain)
    unused_key, key_pull = jax.vjp(lambda inputs, gain_vec: rotate(inputs, gain_vec, positions), key_in, key_gain)
    query_in_grad, query_gain_part = query_pull(query_rot_grad)
    key_in_grad, key_gain_part = key_pull(key_rot_grad)
    rescale = 1.0 / PACKED_TOKENS ** 0.5
    return (query_in_grad.astype(jnp.bfloat16), key_in_grad.astype(jnp.bfloat16), value_grad, query_gain_part * rescale, key_gain_part * rescale)
```

```python
from functools import partial
import math

import jax
import jax.numpy as jnp
from jax import lax
from jax.experimental import pallas as pl
from jax.experimental.pallas import tpu as pltpu
from jax.sharding import PartitionSpec as P

QUERY_SCALAR = 168
REACH = 8
CHUNKS = 4

rope_base = 1000000.0
norm_eps = 1e-06
HIDDEN = -1e30
LOG2E = 1.4426950408889634


def tables(positions, head_size):
    half_dim = head_size // 2
    inverse_freq = rope_base ** (-2.0 * jnp.arange(half_dim, dtype=jnp.float32) / head_size)
    angles = positions.astype(jnp.float32)[:, None] * inverse_freq[None, :]
    return lax.optimization_barrier((jnp.cos(angles), jnp.sin(angles)))


def rotate(inputs, gain_vec, cosine, sine_part):
    meansq = jnp.mean(inputs * inputs, axis=-1, keepdims=True)
    normed = inputs * lax.rsqrt(meansq + norm_eps) * gain_vec
    half_dim = inputs.shape[-1] // 2
    leading = normed[..., :half_dim]
    trailing = normed[..., half_dim:]
    return jnp.concatenate(
        [leading * cosine - trailing * sine_part, trailing * cosine + leading * sine_part], axis=-1
    )


def dot(a, b, dims):
    return lax.dot_general(a, b, (dims, ((), ())), preferred_element_type=jnp.float32)


def attend_kernel(
    factor,
    width,
    info,
    q_ref,
    up_ref,
    k_ref,
    v_ref,
    begin_ref,
    place_ref,
    dq_ref,
    dk_ref,
    dv_ref,
    held_p,
    held_dp,
    held_peak,
    peak_ref,
    total_ref,
    delta_ref,
    dq_acc,
):
    first, own, clear = info[0], info[1], info[2]
    blocks, _, rows, _ = k_ref.shape
    lanes = q_ref.shape[1]
    parts = [pl.ds(at, width) for at in range(0, lanes, width)]
    peak_ref[...] = jnp.full(peak_ref.shape, HIDDEN, jnp.float32)
    total_ref[...] = jnp.zeros(total_ref.shape, jnp.float32)
    delta_ref[...] = jnp.zeros(delta_ref.shape, jnp.float32)
    dq_acc[...] = jnp.zeros(dq_acc.shape, jnp.float32)

    @pl.loop(0, blocks)
    def _(block):
        @pl.when((block < first) | (block > own))
        def _():
            dk_ref[block, 0] = jnp.zeros(dk_ref.shape[2:], dk_ref.dtype)
            dv_ref[block, 0] = jnp.zeros(dv_ref.shape[2:], dv_ref.dtype)

    def forward(block, masked):
        slot = block - first
        key_blk = k_ref[block, 0]
        value_blk = v_ref[block, 0]
        for part in parts:
            scores = dot(key_blk, q_ref[0, part, :], ((1,), (1,))) * (factor * LOG2E)
            attend_grad = dot(value_blk, up_ref[0, part, :], ((1,), (1,)))
            if masked:
                key_at = block * rows + lax.broadcasted_iota(jnp.int32, scores.shape, 0)
                seen = (key_at >= begin_ref[:, part]) & (key_at <= place_ref[:, part])
                scores = jnp.where(seen, scores, HIDDEN)
            old_peak = peak_ref[:, part]
            peak = jnp.maximum(old_peak, jnp.max(scores, axis=0, keepdims=True))
            grown = jnp.exp2(scores - peak)
            shrink = jnp.exp2(old_peak - peak)
            total_ref[:, part] = total_ref[:, part] * shrink + jnp.sum(grown, axis=0, keepdims=True)
            delta_ref[:, part] = delta_ref[:, part] * shrink + jnp.sum(
                grown * attend_grad, axis=0, keepdims=True
            )
            peak_ref[:, part] = peak
            held_peak[slot, :, part] = peak
            held_p[slot, :, part] = grown
            held_dp[slot, :, part] = attend_grad

    @pl.loop(first, own + 1)
    def _(block):
        inside = (block >= clear) & (block < own)

        @pl.when(inside)
        def _():
            forward(block, False)

        @pl.when(jnp.logical_not(inside))
        def _():
            forward(block, True)

    total_ref[...] = 1.0 / total_ref[...]
    delta_ref[...] = delta_ref[...] * total_ref[...]

    @pl.loop(first, own + 1)
    def _(block):
        slot = block - first
        turned_key = k_ref[block, 0].T
        dk = jnp.zeros(dk_ref.shape[2:], jnp.float32)
        dv = jnp.zeros(dv_ref.shape[2:], jnp.float32)
        for part in parts:
            weight = jnp.exp2(held_peak[slot, :, part] - peak_ref[:, part]) * total_ref[:, part]
            attend = held_p[slot, :, part] * weight
            score_grad = (attend * (held_dp[slot, :, part] - delta_ref[:, part])).astype(jnp.bfloat16)
            dv = dv + dot(attend.astype(jnp.bfloat16), up_ref[0, part, :], ((1,), (0,)))
            dk = dk + dot(score_grad, q_ref[0, part, :], ((1,), (0,)))
            dq_acc[:, part] += dot(turned_key, score_grad, ((1,), (0,)))
        dk_ref[block, 0] = (dk * factor).astype(dk_ref.dtype)
        dv_ref[block, 0] = dv.astype(dv_ref.dtype)

    dq_ref[0] = dq_acc[...].T * factor


def attend_grads(info, query_rot, upstream, keys, values, begin, place, reach, factor):
    groups, lanes, head_size = query_rot.shape
    blocks, _, rows, _ = keys.shape
    width = 256 if lanes % 256 == 0 else lanes
    slots = min(reach + 1, blocks)
    own_spec = pl.BlockSpec((1, lanes, head_size), lambda g, info: (g, 0, 0))
    all_spec = pl.BlockSpec((blocks, 1, rows, head_size), lambda g, info: (0, g, 0, 0))
    row_spec = pl.BlockSpec((1, lanes), lambda g, info: (0, 0))
    pairs = groups * lanes * rows * (slots // 2 + 1)
    return pl.pallas_call(
        partial(attend_kernel, factor, width),
        grid_spec=pltpu.PrefetchScalarGridSpec(
            num_scalar_prefetch=1,
            grid=(groups,),
            in_specs=[own_spec, own_spec, all_spec, all_spec, row_spec, row_spec],
            out_specs=[own_spec, all_spec, all_spec],
            scratch_shapes=[
                pltpu.VMEM((slots, rows, lanes), jnp.float32),
                pltpu.VMEM((slots, rows, lanes), jnp.float32),
                pltpu.VMEM((slots, 1, lanes), jnp.float32),
                pltpu.VMEM((1, lanes), jnp.float32),
                pltpu.VMEM((1, lanes), jnp.float32),
                pltpu.VMEM((1, lanes), jnp.float32),
                pltpu.VMEM((head_size, lanes), jnp.float32),
            ],
        ),
        out_shape=(
            jax.ShapeDtypeStruct(query_rot.shape, jnp.float32),
            jax.ShapeDtypeStruct(keys.shape, jnp.bfloat16),
            jax.ShapeDtypeStruct(keys.shape, jnp.bfloat16),
        ),
        compiler_params=pltpu.CompilerParams(
            dimension_semantics=("arbitrary",), vmem_limit_bytes=58 * 1024 * 1024
        ),
        cost_estimate=pl.CostEstimate(
            flops=20 * pairs * head_size,
            transcendentals=pairs,
            bytes_accessed=8 * keys.size + 8 * query_rot.size,
        ),
    )(info, query_rot, upstream, keys, values, begin, place)


def on_device(query_raw, key_raw, values, query_gain, key_gain, documents, upstream):
    block_rows, query_heads, head_size = query_raw.shape
    groups = key_raw.shape[1]
    head_grouping = query_heads // groups
    lanes = head_grouping * block_rows
    factor = QUERY_SCALAR ** (-0.5)
    reach = min(REACH, lax.axis_size("ctx") // 2)
    own = lax.axis_index("ctx").astype(jnp.int32)
    first_row = own * block_rows
    positions = first_row + jnp.arange(block_rows, dtype=jnp.int32)
    cosine, sine_part = tables(positions, head_size)
    chunks = math.gcd(CHUNKS, groups)
    size = groups // chunks

    key_in = jnp.swapaxes(key_raw, 0, 1).astype(jnp.float32)
    key_rot = rotate(key_in, key_gain, cosine, sine_part).astype(jnp.bfloat16)
    value_turned = jnp.swapaxes(values, 0, 1)
    gathered = [
        lax.all_gather(
            jnp.stack([key_rot[at : at + size], value_turned[at : at + size]]), "ctx", axis=0
        )
        for at in range(0, groups, size)
    ]
    query_in = jnp.swapaxes(query_raw, 0, 1).astype(jnp.float32)
    query_rot = (
        rotate(query_in, query_gain, cosine, sine_part)
        .astype(jnp.bfloat16)
        .reshape(groups, lanes, head_size)
    )
    upstream_turned = jnp.swapaxes(upstream, 0, 1).reshape(groups, lanes, head_size)

    own_docs = lax.dynamic_slice_in_dim(documents, first_row, block_rows)
    begin = jnp.sum((documents[None, :] < own_docs[:, None]).astype(jnp.int32), axis=1)
    info = jnp.stack(
        [
            jnp.maximum(begin[0] // block_rows, own - reach),
            own,
            (begin[-1] + block_rows - 1) // block_rows,
        ]
    ).astype(jnp.int32)
    begin_row = jnp.tile(begin, head_grouping)[None, :]
    place_row = jnp.tile(positions, head_grouping)[None, :]

    dq, dk, dv = [], [], []
    for index in range(chunks):
        at = index * size
        dq_part, dk_part, dv_part = attend_grads(
            info,
            query_rot[at : at + size],
            upstream_turned[at : at + size],
            gathered[index][:, 0],
            gathered[index][:, 1],
            begin_row,
            place_row,
            reach,
            factor,
        )
        dq.append(dq_part)
        dk.append(lax.psum_scatter(dk_part, "ctx", scatter_dimension=0))
        dv.append(lax.psum_scatter(dv_part, "ctx", scatter_dimension=0))
    query_rot_grad = jnp.concatenate(dq).reshape(query_heads, block_rows, head_size)
    key_total = jnp.concatenate(dk).astype(jnp.float32)
    value_total = jnp.concatenate(dv)

    turn = lambda inputs, gain_vec: rotate(inputs, gain_vec, cosine, sine_part)
    _, query_pull = jax.vjp(turn, query_in, query_gain)
    _, key_pull = jax.vjp(turn, key_in, key_gain)
    query_in_grad, query_gain_part = query_pull(query_rot_grad)
    key_in_grad, key_gain_part = key_pull(key_total)
    gain_sums = lax.psum(jnp.stack([query_gain_part, key_gain_part]), ("ctx", "tp"))
    rescale = 1.0 / math.sqrt(lax.axis_size("ctx") * block_rows)
    return (
        jnp.swapaxes(query_in_grad.astype(jnp.bfloat16), 0, 1),
        jnp.swapaxes(key_in_grad.astype(jnp.bfloat16), 0, 1),
        jnp.swapaxes(value_total, 0, 1),
        gain_sums[0] * rescale,
        gain_sums[1] * rescale,
    )


def solution(mesh):
    placed = (
        P("ctx", "tp", None),
        P("ctx", "tp", None),
        P("ctx", "tp", None),
        P(),
        P(),
        P(),
        P("ctx", "tp", None),
    )
    return jax.shard_map(
        on_device,
        mesh=mesh,
        in_specs=placed,
        out_specs=(P("ctx", "tp", None), P("ctx", "tp", None), P("ctx", "tp", None), P(), P()),
        check_vma=False,
    )
```

```python
from functools import partial
import math

import jax
import jax.numpy as jnp
from jax import lax
from jax.experimental import pallas as pl
from jax.experimental.pallas import tpu as pltpu
from jax.sharding import PartitionSpec as P

QUERY_SCALAR = 168
REACH = 8
CHUNKS = 4

rope_base = 1000000.0
norm_eps = 1e-06
HIDDEN = -1e30
LOG2E = 1.4426950408889634


def tables(positions, head_size):
    half_dim = head_size // 2
    inverse_freq = rope_base ** (-2.0 * jnp.arange(half_dim, dtype=jnp.float32) / head_size)
    angles = positions.astype(jnp.float32)[:, None] * inverse_freq[None, :]
    return lax.optimization_barrier((jnp.cos(angles), jnp.sin(angles)))


def rotate(inputs, gain_vec, cosine, sine_part):
    meansq = jnp.mean(inputs * inputs, axis=-1, keepdims=True)
    normed = inputs * lax.rsqrt(meansq + norm_eps) * gain_vec
    half_dim = inputs.shape[-1] // 2
    leading = normed[..., :half_dim]
    trailing = normed[..., half_dim:]
    return jnp.concatenate(
        [leading * cosine - trailing * sine_part, trailing * cosine + leading * sine_part], axis=-1
    )


def dot(a, b, dims):
    return lax.dot_general(a, b, (dims, ((), ())), preferred_element_type=jnp.float32)


def attend_kernel(
    factor,
    width,
    info,
    q_ref,
    up_ref,
    k_ref,
    v_ref,
    begin_ref,
    place_ref,
    dq_ref,
    dk_ref,
    dv_ref,
    held_p,
    held_dp,
    held_peak,
    peak_ref,
    total_ref,
    delta_ref,
    dq_acc,
):
    first, own, clear = info[0], info[1], info[2]
    blocks, _, rows, _ = k_ref.shape
    lanes = q_ref.shape[1]
    parts = [pl.ds(at, width) for at in range(0, lanes, width)]
    peak_ref[...] = jnp.full(peak_ref.shape, HIDDEN, jnp.float32)
    total_ref[...] = jnp.zeros(total_ref.shape, jnp.float32)
    delta_ref[...] = jnp.zeros(delta_ref.shape, jnp.float32)
    dq_acc[...] = jnp.zeros(dq_acc.shape, jnp.float32)

    @pl.loop(0, blocks)
    def _(block):
        @pl.when((block < first) | (block > own))
        def _():
            dk_ref[block, 0] = jnp.zeros(dk_ref.shape[2:], dk_ref.dtype)
            dv_ref[block, 0] = jnp.zeros(dv_ref.shape[2:], dv_ref.dtype)

    def forward(block, masked):
        slot = block - first
        key_blk = k_ref[block, 0]
        value_blk = v_ref[block, 0]
        for part in parts:
            scores = dot(key_blk, q_ref[0, part, :], ((1,), (1,))) * (factor * LOG2E)
            attend_grad = dot(value_blk, up_ref[0, part, :], ((1,), (1,)))
            if masked:
                key_at = block * rows + lax.broadcasted_iota(jnp.int32, scores.shape, 0)
                seen = (key_at >= begin_ref[:, part]) & (key_at <= place_ref[:, part])
                scores = jnp.where(seen, scores, HIDDEN)
            old_peak = peak_ref[:, part]
            peak = jnp.maximum(old_peak, jnp.max(scores, axis=0, keepdims=True))
            grown = jnp.exp2(scores - peak)
            shrink = jnp.exp2(old_peak - peak)
            total_ref[:, part] = total_ref[:, part] * shrink + jnp.sum(grown, axis=0, keepdims=True)
            delta_ref[:, part] = delta_ref[:, part] * shrink + jnp.sum(
                grown * attend_grad, axis=0, keepdims=True
            )
            peak_ref[:, part] = peak
            held_peak[slot, :, part] = peak
            held_p[slot, :, part] = grown
            held_dp[slot, :, part] = attend_grad

    @pl.loop(first, own + 1)
    def _(block):
        inside = (block >= clear) & (block < own)

        @pl.when(inside)
        def _():
            forward(block, False)

        @pl.when(jnp.logical_not(inside))
        def _():
            forward(block, True)

    total_ref[...] = 1.0 / total_ref[...]
    delta_ref[...] = delta_ref[...] * total_ref[...]

    @pl.loop(first, own + 1)
    def _(block):
        slot = block - first
        turned_key = k_ref[block, 0].T
        dk = jnp.zeros(dk_ref.shape[2:], jnp.float32)
        dv = jnp.zeros(dv_ref.shape[2:], jnp.float32)
        for part in parts:
            weight = jnp.exp2(held_peak[slot, :, part] - peak_ref[:, part]) * total_ref[:, part]
            attend = held_p[slot, :, part] * weight
            score_grad = (attend * (held_dp[slot, :, part] - delta_ref[:, part])).astype(jnp.bfloat16)
            dv = dv + dot(attend.astype(jnp.bfloat16), up_ref[0, part, :], ((1,), (0,)))
            dk = dk + dot(score_grad, q_ref[0, part, :], ((1,), (0,)))
            dq_acc[:, part] += dot(turned_key, score_grad, ((1,), (0,)))
        dk_ref[block, 0] = (dk * factor).astype(dk_ref.dtype)
        dv_ref[block, 0] = dv.astype(dv_ref.dtype)

    dq_ref[0] = dq_acc[...].T * factor


def heads_kernel(
    factor,
    q_tile,
    k_tile,
    width,
    info,
    got_ref,
    begin_ref,
    out_ref,
    q_all,
    up_all,
    k_all,
    v_all,
    dq_all,
    dk_all,
    dv_all,
    held_p,
    held_dp,
    held_peak,
    peak_ref,
    total_ref,
    delta_ref,
    dq_acc,
):
    blocks, _, _, rows, head_size = got_ref.shape
    parts = [pl.ds(at, width) for at in range(0, q_tile, width)]

    @pl.loop(0, blocks)
    def _(block):
        span = pl.ds(pl.multiple_of(block * rows, rows), rows)
        for which, whole in enumerate((q_all, up_all, k_all, v_all)):
            whole[span, :] = got_ref[block, 0, which]
        dk_all[span, :] = jnp.zeros((rows, head_size), jnp.float32)
        dv_all[span, :] = jnp.zeros((rows, head_size), jnp.float32)

    @pl.loop(0, blocks * rows // q_tile)
    def _(tile):
        first, clear = info[0, tile], info[1, tile]
        start = pl.multiple_of(tile * q_tile, q_tile)
        final = (start + q_tile - 1) // k_tile
        full = start // k_tile
        peak_ref[...] = jnp.full(peak_ref.shape, HIDDEN, jnp.float32)
        total_ref[...] = jnp.zeros(total_ref.shape, jnp.float32)
        delta_ref[...] = jnp.zeros(delta_ref.shape, jnp.float32)
        dq_acc[...] = jnp.zeros(dq_acc.shape, jnp.float32)

        def queries(part):
            return pl.ds(pl.multiple_of(start + part.start, width), width)

        def forward(block, masked):
            slot = block - first
            span = pl.ds(pl.multiple_of(block * k_tile, k_tile), k_tile)
            key_blk = k_all[span, :]
            value_blk = v_all[span, :]
            for part in parts:
                scores = dot(key_blk, q_all[queries(part), :], ((1,), (1,))) * (factor * LOG2E)
                attend_grad = dot(value_blk, up_all[queries(part), :], ((1,), (1,)))
                if masked:
                    key_at = block * k_tile + lax.broadcasted_iota(jnp.int32, scores.shape, 0)
                    place = start + part.start + lax.broadcasted_iota(jnp.int32, scores.shape, 1)
                    seen = (key_at >= begin_ref[tile, :, part]) & (key_at <= place)
                    scores = jnp.where(seen, scores, HIDDEN)
                old_peak = peak_ref[:, part]
                peak = jnp.maximum(old_peak, jnp.max(scores, axis=0, keepdims=True))
                grown = jnp.exp2(scores - peak)
                shrink = jnp.exp2(old_peak - peak)
                total_ref[:, part] = total_ref[:, part] * shrink + jnp.sum(
                    grown, axis=0, keepdims=True
                )
                delta_ref[:, part] = delta_ref[:, part] * shrink + jnp.sum(
                    grown * attend_grad, axis=0, keepdims=True
                )
                peak_ref[:, part] = peak
                held_peak[slot, :, part] = peak
                held_p[slot, :, part] = grown
                held_dp[slot, :, part] = attend_grad

        @pl.loop(first, final + 1)
        def _(block):
            inside = (block >= clear) & (block < full)

            @pl.when(inside)
            def _():
                forward(block, False)

            @pl.when(jnp.logical_not(inside))
            def _():
                forward(block, True)

        total_ref[...] = 1.0 / total_ref[...]
        delta_ref[...] = delta_ref[...] * total_ref[...]

        @pl.loop(first, final + 1)
        def _(block):
            slot = block - first
            span = pl.ds(pl.multiple_of(block * k_tile, k_tile), k_tile)
            turned_key = k_all[span, :].T
            dk = dk_all[span, :]
            dv = dv_all[span, :]
            for part in parts:
                weight = jnp.exp2(held_peak[slot, :, part] - peak_ref[:, part]) * total_ref[:, part]
                attend = held_p[slot, :, part] * weight
                score_grad = (attend * (held_dp[slot, :, part] - delta_ref[:, part])).astype(
                    jnp.bfloat16
                )
                dv = dv + dot(attend.astype(jnp.bfloat16), up_all[queries(part), :], ((1,), (0,)))
                dk = dk + dot(score_grad, q_all[queries(part), :], ((1,), (0,)))
                dq_acc[:, part] += dot(turned_key, score_grad, ((1,), (0,)))
            dk_all[span, :] = dk
            dv_all[span, :] = dv

        dq_all[pl.ds(start, q_tile), :] = dq_acc[...].T

    @pl.loop(0, blocks)
    def _(block):
        span = pl.ds(pl.multiple_of(block * rows, rows), rows)
        out_ref[block, 0, 0] = (dq_all[span, :] * factor).astype(out_ref.dtype)
        out_ref[block, 0, 1] = (dk_all[span, :] * factor).astype(out_ref.dtype)
        out_ref[block, 0, 2] = dv_all[span, :].astype(out_ref.dtype)


def heads_grads(got, documents, reach, factor):
    blocks, heads, _, rows, head_size = got.shape
    tokens = blocks * rows
    q_tile = 512 if tokens % 512 == 0 else rows
    k_tile = 256 if tokens % 256 == 0 else rows
    width = 256 if q_tile % 256 == 0 else q_tile
    slots = min((reach * rows + q_tile - 2) // k_tile + 2, tokens // k_tile)
    inner = math.gcd(tokens, 128)
    at = jnp.arange(tokens, dtype=jnp.int32)
    earlier = jnp.concatenate([documents[:1], documents[:-1]])
    opened = jnp.where(documents != earlier, at, 0).reshape(-1, inner)
    lane = jnp.arange(inner)
    group = jnp.arange(tokens // inner)
    within = jnp.max(jnp.where(lane[None, :] <= lane[:, None], opened[:, None, :], 0), axis=-1)
    tops = jnp.max(opened, axis=1)
    before = jnp.max(jnp.where(group[None, :] < group[:, None], tops[None, :], 0), axis=-1)
    begin = jnp.maximum(within, before[:, None]).reshape(-1, q_tile)
    starts = jnp.arange(tokens // q_tile, dtype=jnp.int32) * q_tile
    lowest = jnp.maximum(begin[:, 0], starts - reach * rows + 1)
    info = jnp.stack([lowest // k_tile, (begin[:, -1] + k_tile - 1) // k_tile])
    info = info.astype(jnp.int32)
    got_spec = pl.BlockSpec((blocks, 1, 4, rows, head_size), lambda g, info: (0, g, 0, 0, 0))
    out_spec = pl.BlockSpec((blocks, 1, 3, rows, head_size), lambda g, info: (0, g, 0, 0, 0))
    begin_spec = pl.BlockSpec((tokens // q_tile, 1, q_tile), lambda g, info: (0, 0, 0))
    whole = pltpu.VMEM((tokens, head_size), jnp.bfloat16)
    total = pltpu.VMEM((tokens, head_size), jnp.float32)
    row = pltpu.VMEM((1, q_tile), jnp.float32)
    return pl.pallas_call(
        partial(heads_kernel, factor, q_tile, k_tile, width),
        grid_spec=pltpu.PrefetchScalarGridSpec(
            num_scalar_prefetch=1,
            grid=(heads,),
            in_specs=[got_spec, begin_spec],
            out_specs=out_spec,
            scratch_shapes=[whole] * 4
            + [total] * 3
            + [pltpu.VMEM((slots, k_tile, q_tile), jnp.float32)] * 2
            + [pltpu.VMEM((slots, 1, q_tile), jnp.float32)]
            + [row] * 3
            + [pltpu.VMEM((head_size, q_tile), jnp.float32)],
        ),
        out_shape=jax.ShapeDtypeStruct((blocks, heads, 3, rows, head_size), jnp.bfloat16),
        compiler_params=pltpu.CompilerParams(
            dimension_semantics=("arbitrary",), vmem_limit_bytes=60 * 1024 * 1024
        ),
    )(info, got, begin[:, None, :])


def attend_grads(info, query_rot, upstream, keys, values, begin, place, reach, factor):
    groups, lanes, head_size = query_rot.shape
    blocks, _, rows, _ = keys.shape
    width = 256 if lanes % 256 == 0 else lanes
    slots = min(reach + 1, blocks)
    own_spec = pl.BlockSpec((1, lanes, head_size), lambda g, info: (g, 0, 0))
    all_spec = pl.BlockSpec((blocks, 1, rows, head_size), lambda g, info: (0, g, 0, 0))
    row_spec = pl.BlockSpec((1, lanes), lambda g, info: (0, 0))
    pairs = groups * lanes * rows * (slots // 2 + 1)
    return pl.pallas_call(
        partial(attend_kernel, factor, width),
        grid_spec=pltpu.PrefetchScalarGridSpec(
            num_scalar_prefetch=1,
            grid=(groups,),
            in_specs=[own_spec, own_spec, all_spec, all_spec, row_spec, row_spec],
            out_specs=[own_spec, all_spec, all_spec],
            scratch_shapes=[
                pltpu.VMEM((slots, rows, lanes), jnp.float32),
                pltpu.VMEM((slots, rows, lanes), jnp.float32),
                pltpu.VMEM((slots, 1, lanes), jnp.float32),
                pltpu.VMEM((1, lanes), jnp.float32),
                pltpu.VMEM((1, lanes), jnp.float32),
                pltpu.VMEM((1, lanes), jnp.float32),
                pltpu.VMEM((head_size, lanes), jnp.float32),
            ],
        ),
        out_shape=(
            jax.ShapeDtypeStruct(query_rot.shape, jnp.float32),
            jax.ShapeDtypeStruct(keys.shape, jnp.bfloat16),
            jax.ShapeDtypeStruct(keys.shape, jnp.bfloat16),
        ),
        compiler_params=pltpu.CompilerParams(
            dimension_semantics=("arbitrary",), vmem_limit_bytes=58 * 1024 * 1024
        ),
        cost_estimate=pl.CostEstimate(
            flops=20 * pairs * head_size,
            transcendentals=pairs,
            bytes_accessed=8 * keys.size + 8 * query_rot.size,
        ),
    )(info, query_rot, upstream, keys, values, begin, place)


def on_device(query_raw, key_raw, values, query_gain, key_gain, documents, upstream):
    block_rows, query_heads, head_size = query_raw.shape
    groups = key_raw.shape[1]
    head_grouping = query_heads // groups
    lanes = head_grouping * block_rows
    factor = QUERY_SCALAR ** (-0.5)
    reach = min(REACH, lax.axis_size("ctx") // 2)
    own = lax.axis_index("ctx").astype(jnp.int32)
    first_row = own * block_rows
    positions = first_row + jnp.arange(block_rows, dtype=jnp.int32)
    cosine, sine_part = tables(positions, head_size)
    chunks = math.gcd(CHUNKS, groups)
    size = groups // chunks

    key_in = jnp.swapaxes(key_raw, 0, 1).astype(jnp.float32)
    key_rot = rotate(key_in, key_gain, cosine, sine_part).astype(jnp.bfloat16)
    value_turned = jnp.swapaxes(values, 0, 1)
    query_in = jnp.swapaxes(query_raw, 0, 1).astype(jnp.float32)
    query_rot = (
        rotate(query_in, query_gain, cosine, sine_part)
        .astype(jnp.bfloat16)
        .reshape(groups, lanes, head_size)
    )
    upstream_turned = jnp.swapaxes(upstream, 0, 1).reshape(groups, lanes, head_size)

    devices = lax.axis_size("ctx")
    if query_heads % devices == 0:
        heads = query_heads // devices
        sent = jnp.stack(
            [
                query_rot.reshape(query_heads, block_rows, head_size),
                jnp.swapaxes(upstream, 0, 1),
                jnp.repeat(key_rot, head_grouping, axis=0),
                jnp.repeat(value_turned, head_grouping, axis=0),
            ],
            axis=1,
        )
        got = lax.all_to_all(sent, "ctx", 0, 0, tiled=True)
        made = heads_grads(
            got.reshape(devices, heads, 4, block_rows, head_size), documents, reach, factor
        )
        back = lax.all_to_all(
            made.reshape(query_heads, 3, block_rows, head_size), "ctx", 0, 0, tiled=True
        )
        query_rot_grad = back[:, 0].astype(jnp.float32)
        shared = back.reshape(groups, head_grouping, 3, block_rows, head_size)
        key_total = jnp.sum(shared[:, :, 1].astype(jnp.float32), axis=1)
        value_total = jnp.sum(shared[:, :, 2].astype(jnp.float32), axis=1).astype(jnp.bfloat16)
    else:
        gathered = [
            lax.all_gather(
                jnp.stack([key_rot[at : at + size], value_turned[at : at + size]]), "ctx", axis=0
            )
            for at in range(0, groups, size)
        ]
        own_docs = lax.dynamic_slice_in_dim(documents, first_row, block_rows)
        begin = jnp.sum((documents[None, :] < own_docs[:, None]).astype(jnp.int32), axis=1)
        info = jnp.stack(
            [
                jnp.maximum(begin[0] // block_rows, own - reach),
                own,
                (begin[-1] + block_rows - 1) // block_rows,
            ]
        ).astype(jnp.int32)
        begin_row = jnp.tile(begin, head_grouping)[None, :]
        place_row = jnp.tile(positions, head_grouping)[None, :]

        dq, dk, dv = [], [], []
        for index in range(chunks):
            at = index * size
            dq_part, dk_part, dv_part = attend_grads(
                info,
                query_rot[at : at + size],
                upstream_turned[at : at + size],
                gathered[index][:, 0],
                gathered[index][:, 1],
                begin_row,
                place_row,
                reach,
                factor,
            )
            dq.append(dq_part)
            dk.append(lax.psum_scatter(dk_part, "ctx", scatter_dimension=0))
            dv.append(lax.psum_scatter(dv_part, "ctx", scatter_dimension=0))
        query_rot_grad = jnp.concatenate(dq).reshape(query_heads, block_rows, head_size)
        key_total = jnp.concatenate(dk).astype(jnp.float32)
        value_total = jnp.concatenate(dv)


    turn = lambda inputs, gain_vec: rotate(inputs, gain_vec, cosine, sine_part)
    _, query_pull = jax.vjp(turn, query_in, query_gain)
    _, key_pull = jax.vjp(turn, key_in, key_gain)
    query_in_grad, query_gain_part = query_pull(query_rot_grad)
    key_in_grad, key_gain_part = key_pull(key_total)
    gain_sums = lax.psum(jnp.stack([query_gain_part, key_gain_part]), ("ctx", "tp"))
    rescale = 1.0 / math.sqrt(lax.axis_size("ctx") * block_rows)
    return (
        jnp.swapaxes(query_in_grad.astype(jnp.bfloat16), 0, 1),
        jnp.swapaxes(key_in_grad.astype(jnp.bfloat16), 0, 1),
        jnp.swapaxes(value_total, 0, 1),
        gain_sums[0] * rescale,
        gain_sums[1] * rescale,
    )


def solution(mesh):
    placed = (
        P("ctx", "tp", None),
        P("ctx", "tp", None),
        P("ctx", "tp", None),
        P(),
        P(),
        P(),
        P("ctx", "tp", None),
    )
    return jax.shard_map(
        on_device,
        mesh=mesh,
        in_specs=placed,
        out_specs=(P("ctx", "tp", None), P("ctx", "tp", None), P("ctx", "tp", None), P(), P()),
        check_vma=False,
    )
```

```python
from functools import partial
import math

import jax
import jax.numpy as jnp
from jax import lax
from jax.experimental import pallas as pl
from jax.experimental.pallas import tpu as pltpu
from jax.sharding import PartitionSpec as P

QUERY_SCALAR = 168
REACH = 8
CHUNKS = 4

rope_base = 1000000.0
norm_eps = 1e-06
HIDDEN = -1e30
LOG2E = 1.4426950408889634


def tables(positions, head_size):
    half_dim = head_size // 2
    inverse_freq = rope_base ** (-2.0 * jnp.arange(half_dim, dtype=jnp.float32) / head_size)
    angles = positions.astype(jnp.float32)[:, None] * inverse_freq[None, :]
    return lax.optimization_barrier((jnp.cos(angles), jnp.sin(angles)))


def rotate(inputs, gain_vec, cosine, sine_part):
    meansq = jnp.mean(inputs * inputs, axis=-1, keepdims=True)
    normed = inputs * lax.rsqrt(meansq + norm_eps) * gain_vec
    half_dim = inputs.shape[-1] // 2
    leading = normed[..., :half_dim]
    trailing = normed[..., half_dim:]
    return jnp.concatenate(
        [leading * cosine - trailing * sine_part, trailing * cosine + leading * sine_part], axis=-1
    )


def dot(a, b, dims):
    return lax.dot_general(a, b, (dims, ((), ())), preferred_element_type=jnp.float32)


def attend_kernel(
    factor,
    width,
    info,
    q_ref,
    up_ref,
    k_ref,
    v_ref,
    begin_ref,
    place_ref,
    dq_ref,
    dk_ref,
    dv_ref,
    held_p,
    held_dp,
    held_peak,
    peak_ref,
    total_ref,
    delta_ref,
    dq_acc,
):
    first, own, clear = info[0], info[1], info[2]
    blocks, _, rows, _ = k_ref.shape
    lanes = q_ref.shape[1]
    parts = [pl.ds(at, width) for at in range(0, lanes, width)]
    peak_ref[...] = jnp.full(peak_ref.shape, HIDDEN, jnp.float32)
    total_ref[...] = jnp.zeros(total_ref.shape, jnp.float32)
    delta_ref[...] = jnp.zeros(delta_ref.shape, jnp.float32)
    dq_acc[...] = jnp.zeros(dq_acc.shape, jnp.float32)

    @pl.loop(0, blocks)
    def _(block):
        @pl.when((block < first) | (block > own))
        def _():
            dk_ref[block, 0] = jnp.zeros(dk_ref.shape[2:], dk_ref.dtype)
            dv_ref[block, 0] = jnp.zeros(dv_ref.shape[2:], dv_ref.dtype)

    def forward(block, masked):
        slot = block - first
        key_blk = k_ref[block, 0]
        value_blk = v_ref[block, 0]
        for part in parts:
            scores = dot(key_blk, q_ref[0, part, :], ((1,), (1,))) * (factor * LOG2E)
            attend_grad = dot(value_blk, up_ref[0, part, :], ((1,), (1,)))
            if masked:
                key_at = block * rows + lax.broadcasted_iota(jnp.int32, scores.shape, 0)
                seen = (key_at >= begin_ref[:, part]) & (key_at <= place_ref[:, part])
                scores = jnp.where(seen, scores, HIDDEN)
            old_peak = peak_ref[:, part]
            peak = jnp.maximum(old_peak, jnp.max(scores, axis=0, keepdims=True))
            grown = jnp.exp2(scores - peak)
            shrink = jnp.exp2(old_peak - peak)
            total_ref[:, part] = total_ref[:, part] * shrink + jnp.sum(grown, axis=0, keepdims=True)
            delta_ref[:, part] = delta_ref[:, part] * shrink + jnp.sum(
                grown * attend_grad, axis=0, keepdims=True
            )
            peak_ref[:, part] = peak
            held_peak[slot, :, part] = peak
            held_p[slot, :, part] = grown
            held_dp[slot, :, part] = attend_grad

    @pl.loop(first, own + 1)
    def _(block):
        inside = (block >= clear) & (block < own)

        @pl.when(inside)
        def _():
            forward(block, False)

        @pl.when(jnp.logical_not(inside))
        def _():
            forward(block, True)

    total_ref[...] = 1.0 / total_ref[...]
    delta_ref[...] = delta_ref[...] * total_ref[...]

    @pl.loop(first, own + 1)
    def _(block):
        slot = block - first
        turned_key = k_ref[block, 0].T
        dk = jnp.zeros(dk_ref.shape[2:], jnp.float32)
        dv = jnp.zeros(dv_ref.shape[2:], jnp.float32)
        for part in parts:
            weight = jnp.exp2(held_peak[slot, :, part] - peak_ref[:, part]) * total_ref[:, part]
            attend = held_p[slot, :, part] * weight
            score_grad = (attend * (held_dp[slot, :, part] - delta_ref[:, part])).astype(jnp.bfloat16)
            dv = dv + dot(attend.astype(jnp.bfloat16), up_ref[0, part, :], ((1,), (0,)))
            dk = dk + dot(score_grad, q_ref[0, part, :], ((1,), (0,)))
            dq_acc[:, part] += dot(turned_key, score_grad, ((1,), (0,)))
        dk_ref[block, 0] = (dk * factor).astype(dk_ref.dtype)
        dv_ref[block, 0] = dv.astype(dv_ref.dtype)

    dq_ref[0] = dq_acc[...].T * factor


def heads_kernel(
    factor,
    q_tile,
    k_tile,
    width,
    info,
    got_ref,
    other_ref,
    begin_ref,
    out_ref,
    give_ref,
    q_all,
    up_all,
    k_all,
    v_all,
    dq_all,
    dk_all,
    dv_all,
    held_p,
    held_dp,
    held_peak,
    peak_ref,
    total_ref,
    delta_ref,
    dq_acc,
):
    blocks, _, _, rows, head_size = got_ref.shape
    parts = [pl.ds(at, width) for at in range(0, q_tile, width)]

    @pl.loop(0, blocks)
    def _(block):
        span = pl.ds(pl.multiple_of(block * rows, rows), rows)
        q_all[span, :] = got_ref[block, 0, 0]
        up_all[span, :] = got_ref[block, 0, 1]

        @pl.when(info[2, 0] == 0)
        def _():
            k_all[span, :] = got_ref[block, 0, 2]
            v_all[span, :] = other_ref[block]

        @pl.when(info[2, 0] != 0)
        def _():
            k_all[span, :] = other_ref[block]
            v_all[span, :] = got_ref[block, 0, 2]

        dk_all[span, :] = jnp.zeros((rows, head_size), jnp.float32)
        dv_all[span, :] = jnp.zeros((rows, head_size), jnp.float32)

    @pl.loop(0, blocks * rows // q_tile)
    def _(tile):
        first, clear = info[0, tile], info[1, tile]
        start = pl.multiple_of(tile * q_tile, q_tile)
        final = (start + q_tile - 1) // k_tile
        full = start // k_tile
        peak_ref[...] = jnp.full(peak_ref.shape, HIDDEN, jnp.float32)
        total_ref[...] = jnp.zeros(total_ref.shape, jnp.float32)
        delta_ref[...] = jnp.zeros(delta_ref.shape, jnp.float32)
        dq_acc[...] = jnp.zeros(dq_acc.shape, jnp.float32)

        def queries(part):
            return pl.ds(pl.multiple_of(start + part.start, width), width)

        def forward(block, masked):
            slot = block - first
            span = pl.ds(pl.multiple_of(block * k_tile, k_tile), k_tile)
            key_blk = k_all[span, :]
            value_blk = v_all[span, :]
            for part in parts:
                scores = dot(key_blk, q_all[queries(part), :], ((1,), (1,))) * (factor * LOG2E)
                attend_grad = dot(value_blk, up_all[queries(part), :], ((1,), (1,)))
                if masked:
                    key_at = block * k_tile + lax.broadcasted_iota(jnp.int32, scores.shape, 0)
                    place = start + part.start + lax.broadcasted_iota(jnp.int32, scores.shape, 1)
                    seen = (key_at >= begin_ref[tile, :, part]) & (key_at <= place)
                    scores = jnp.where(seen, scores, HIDDEN)
                old_peak = peak_ref[:, part]
                peak = jnp.maximum(old_peak, jnp.max(scores, axis=0, keepdims=True))
                grown = jnp.exp2(scores - peak)
                shrink = jnp.exp2(old_peak - peak)
                total_ref[:, part] = total_ref[:, part] * shrink + jnp.sum(
                    grown, axis=0, keepdims=True
                )
                delta_ref[:, part] = delta_ref[:, part] * shrink + jnp.sum(
                    grown * attend_grad, axis=0, keepdims=True
                )
                peak_ref[:, part] = peak
                held_peak[slot, :, part] = peak
                held_p[slot, :, part] = grown
                held_dp[slot, :, part] = attend_grad

        @pl.loop(first, final + 1)
        def _(block):
            inside = (block >= clear) & (block < full)

            @pl.when(inside)
            def _():
                forward(block, False)

            @pl.when(jnp.logical_not(inside))
            def _():
                forward(block, True)

        total_ref[...] = 1.0 / total_ref[...]
        delta_ref[...] = delta_ref[...] * total_ref[...]

        @pl.loop(first, final + 1)
        def _(block):
            slot = block - first
            span = pl.ds(pl.multiple_of(block * k_tile, k_tile), k_tile)
            turned_key = k_all[span, :].T
            dk = dk_all[span, :]
            dv = dv_all[span, :]
            for part in parts:
                weight = jnp.exp2(held_peak[slot, :, part] - peak_ref[:, part]) * total_ref[:, part]
                attend = held_p[slot, :, part] * weight
                score_grad = (attend * (held_dp[slot, :, part] - delta_ref[:, part])).astype(
                    jnp.bfloat16
                )
                dv = dv + dot(attend.astype(jnp.bfloat16), up_all[queries(part), :], ((1,), (0,)))
                dk = dk + dot(score_grad, q_all[queries(part), :], ((1,), (0,)))
                dq_acc[:, part] += dot(turned_key, score_grad, ((1,), (0,)))
            dk_all[span, :] = dk
            dv_all[span, :] = dv

        dq_all[pl.ds(start, q_tile), :] = dq_acc[...].T

    @pl.loop(0, blocks)
    def _(block):
        span = pl.ds(pl.multiple_of(block * rows, rows), rows)
        out_ref[block, 0, 0] = (dq_all[span, :] * factor).astype(out_ref.dtype)
        dk = (dk_all[span, :] * factor).astype(out_ref.dtype)
        dv = dv_all[span, :].astype(out_ref.dtype)

        @pl.when(info[2, 0] == 0)
        def _():
            out_ref[block, 0, 1] = dk
            give_ref[block] = dv

        @pl.when(info[2, 0] != 0)
        def _():
            out_ref[block, 0, 1] = dv
            give_ref[block] = dk


def heads_grads(got, other, parity, documents, reach, factor):
    blocks, heads, _, rows, head_size = got.shape
    tokens = blocks * rows
    q_tile = 512 if tokens % 512 == 0 else rows
    k_tile = 256 if tokens % 256 == 0 else rows
    width = 256 if q_tile % 256 == 0 else q_tile
    slots = min((reach * rows + q_tile - 2) // k_tile + 2, tokens // k_tile)
    inner = math.gcd(tokens, 128)
    at = jnp.arange(tokens, dtype=jnp.int32)
    earlier = jnp.concatenate([documents[:1], documents[:-1]])
    opened = jnp.where(documents != earlier, at, 0).reshape(-1, inner)
    lane = jnp.arange(inner)
    group = jnp.arange(tokens // inner)
    within = jnp.max(jnp.where(lane[None, :] <= lane[:, None], opened[:, None, :], 0), axis=-1)
    tops = jnp.max(opened, axis=1)
    before = jnp.max(jnp.where(group[None, :] < group[:, None], tops[None, :], 0), axis=-1)
    begin = jnp.maximum(within, before[:, None]).reshape(-1, q_tile)
    starts = jnp.arange(tokens // q_tile, dtype=jnp.int32) * q_tile
    lowest = jnp.maximum(begin[:, 0], starts - reach * rows + 1)
    info = jnp.stack(
        [
            lowest // k_tile,
            (begin[:, -1] + k_tile - 1) // k_tile,
            jnp.full(starts.shape, parity, jnp.int32),
        ]
    )
    info = info.astype(jnp.int32)
    got_spec = pl.BlockSpec((blocks, 1, 3, rows, head_size), lambda g, info: (0, g, 0, 0, 0))
    other_spec = pl.BlockSpec((blocks, rows, head_size), lambda g, info: (0, 0, 0))
    out_spec = pl.BlockSpec((blocks, 1, 2, rows, head_size), lambda g, info: (0, g, 0, 0, 0))
    begin_spec = pl.BlockSpec((tokens // q_tile, 1, q_tile), lambda g, info: (0, 0, 0))
    whole = pltpu.VMEM((tokens, head_size), jnp.bfloat16)
    total = pltpu.VMEM((tokens, head_size), jnp.float32)
    row = pltpu.VMEM((1, q_tile), jnp.float32)
    return pl.pallas_call(
        partial(heads_kernel, factor, q_tile, k_tile, width),
        grid_spec=pltpu.PrefetchScalarGridSpec(
            num_scalar_prefetch=1,
            grid=(heads,),
            in_specs=[got_spec, other_spec, begin_spec],
            out_specs=[out_spec, other_spec],
            scratch_shapes=[whole] * 4
            + [total] * 3
            + [pltpu.VMEM((slots, k_tile, q_tile), jnp.float32)] * 2
            + [pltpu.VMEM((slots, 1, q_tile), jnp.float32)]
            + [row] * 3
            + [pltpu.VMEM((head_size, q_tile), jnp.float32)],
        ),
        out_shape=(
            jax.ShapeDtypeStruct((blocks, heads, 2, rows, head_size), jnp.bfloat16),
            jax.ShapeDtypeStruct(other.shape, jnp.bfloat16),
        ),
        compiler_params=pltpu.CompilerParams(
            dimension_semantics=("arbitrary",), vmem_limit_bytes=60 * 1024 * 1024
        ),
    )(info, got, other, begin[:, None, :])


def attend_grads(info, query_rot, upstream, keys, values, begin, place, reach, factor):
    groups, lanes, head_size = query_rot.shape
    blocks, _, rows, _ = keys.shape
    width = 256 if lanes % 256 == 0 else lanes
    slots = min(reach + 1, blocks)
    own_spec = pl.BlockSpec((1, lanes, head_size), lambda g, info: (g, 0, 0))
    all_spec = pl.BlockSpec((blocks, 1, rows, head_size), lambda g, info: (0, g, 0, 0))
    row_spec = pl.BlockSpec((1, lanes), lambda g, info: (0, 0))
    pairs = groups * lanes * rows * (slots // 2 + 1)
    return pl.pallas_call(
        partial(attend_kernel, factor, width),
        grid_spec=pltpu.PrefetchScalarGridSpec(
            num_scalar_prefetch=1,
            grid=(groups,),
            in_specs=[own_spec, own_spec, all_spec, all_spec, row_spec, row_spec],
            out_specs=[own_spec, all_spec, all_spec],
            scratch_shapes=[
                pltpu.VMEM((slots, rows, lanes), jnp.float32),
                pltpu.VMEM((slots, rows, lanes), jnp.float32),
                pltpu.VMEM((slots, 1, lanes), jnp.float32),
                pltpu.VMEM((1, lanes), jnp.float32),
                pltpu.VMEM((1, lanes), jnp.float32),
                pltpu.VMEM((1, lanes), jnp.float32),
                pltpu.VMEM((head_size, lanes), jnp.float32),
            ],
        ),
        out_shape=(
            jax.ShapeDtypeStruct(query_rot.shape, jnp.float32),
            jax.ShapeDtypeStruct(keys.shape, jnp.bfloat16),
            jax.ShapeDtypeStruct(keys.shape, jnp.bfloat16),
        ),
        compiler_params=pltpu.CompilerParams(
            dimension_semantics=("arbitrary",), vmem_limit_bytes=58 * 1024 * 1024
        ),
        cost_estimate=pl.CostEstimate(
            flops=20 * pairs * head_size,
            transcendentals=pairs,
            bytes_accessed=8 * keys.size + 8 * query_rot.size,
        ),
    )(info, query_rot, upstream, keys, values, begin, place)


def on_device(query_raw, key_raw, values, query_gain, key_gain, documents, upstream):
    block_rows, query_heads, head_size = query_raw.shape
    groups = key_raw.shape[1]
    head_grouping = query_heads // groups
    lanes = head_grouping * block_rows
    factor = QUERY_SCALAR ** (-0.5)
    reach = min(REACH, lax.axis_size("ctx") // 2)
    own = lax.axis_index("ctx").astype(jnp.int32)
    first_row = own * block_rows
    positions = first_row + jnp.arange(block_rows, dtype=jnp.int32)
    cosine, sine_part = tables(positions, head_size)
    chunks = math.gcd(CHUNKS, groups)
    size = groups // chunks

    key_in = jnp.swapaxes(key_raw, 0, 1).astype(jnp.float32)
    key_rot = rotate(key_in, key_gain, cosine, sine_part).astype(jnp.bfloat16)
    value_turned = jnp.swapaxes(values, 0, 1)
    query_in = jnp.swapaxes(query_raw, 0, 1).astype(jnp.float32)
    query_rot = (
        rotate(query_in, query_gain, cosine, sine_part)
        .astype(jnp.bfloat16)
        .reshape(groups, lanes, head_size)
    )
    upstream_turned = jnp.swapaxes(upstream, 0, 1).reshape(groups, lanes, head_size)

    devices = lax.axis_size("ctx")
    if query_heads == devices and head_grouping == 2:
        swap = [(index, index ^ 1) for index in range(devices)]
        halves = jnp.stack([key_rot, value_turned], axis=1)
        sent = jnp.stack(
            [
                query_rot.reshape(query_heads, block_rows, head_size),
                jnp.swapaxes(upstream, 0, 1),
                halves.reshape(query_heads, block_rows, head_size),
            ],
            axis=1,
        )
        got = lax.all_to_all(sent, "ctx", 0, 0, tiled=True)
        other = lax.ppermute(got[:, 2], "ctx", swap)
        made, give = heads_grads(got[:, None], other, own % 2, documents, reach, factor)
        taken = lax.ppermute(give, "ctx", swap)
        summed = (made[:, 0, 1].astype(jnp.float32) + taken.astype(jnp.float32)).astype(jnp.bfloat16)
        back = lax.all_to_all(
            jnp.stack([made[:, 0, 0], summed], axis=1), "ctx", 0, 0, tiled=True
        )
        query_rot_grad = back[:, 0].astype(jnp.float32)
        shared = back[:, 1].reshape(groups, 2, block_rows, head_size)
        key_total = shared[:, 0].astype(jnp.float32)
        value_total = shared[:, 1]
    else:
        gathered = [
            lax.all_gather(
                jnp.stack([key_rot[at : at + size], value_turned[at : at + size]]), "ctx", axis=0
            )
            for at in range(0, groups, size)
        ]
        own_docs = lax.dynamic_slice_in_dim(documents, first_row, block_rows)
        begin = jnp.sum((documents[None, :] < own_docs[:, None]).astype(jnp.int32), axis=1)
        info = jnp.stack(
            [
                jnp.maximum(begin[0] // block_rows, own - reach),
                own,
                (begin[-1] + block_rows - 1) // block_rows,
            ]
        ).astype(jnp.int32)
        begin_row = jnp.tile(begin, head_grouping)[None, :]
        place_row = jnp.tile(positions, head_grouping)[None, :]

        dq, dk, dv = [], [], []
        for index in range(chunks):
            at = index * size
            dq_part, dk_part, dv_part = attend_grads(
                info,
                query_rot[at : at + size],
                upstream_turned[at : at + size],
                gathered[index][:, 0],
                gathered[index][:, 1],
                begin_row,
                place_row,
                reach,
                factor,
            )
            dq.append(dq_part)
            dk.append(lax.psum_scatter(dk_part, "ctx", scatter_dimension=0))
            dv.append(lax.psum_scatter(dv_part, "ctx", scatter_dimension=0))
        query_rot_grad = jnp.concatenate(dq).reshape(query_heads, block_rows, head_size)
        key_total = jnp.concatenate(dk).astype(jnp.float32)
        value_total = jnp.concatenate(dv)


    turn = lambda inputs, gain_vec: rotate(inputs, gain_vec, cosine, sine_part)
    _, query_pull = jax.vjp(turn, query_in, query_gain)
    _, key_pull = jax.vjp(turn, key_in, key_gain)
    query_in_grad, query_gain_part = query_pull(query_rot_grad)
    key_in_grad, key_gain_part = key_pull(key_total)
    parts = jnp.stack([query_gain_part, key_gain_part])
    everyone = lax.axis_size("ctx") * lax.axis_size("tp")
    spread = jnp.broadcast_to(parts[None], (everyone,) + parts.shape)
    gain_sums = jnp.sum(lax.all_to_all(spread, ("ctx", "tp"), 0, 0, tiled=True), axis=0)
    rescale = 1.0 / math.sqrt(lax.axis_size("ctx") * block_rows)
    return (
        jnp.swapaxes(query_in_grad.astype(jnp.bfloat16), 0, 1),
        jnp.swapaxes(key_in_grad.astype(jnp.bfloat16), 0, 1),
        jnp.swapaxes(value_total, 0, 1),
        gain_sums[0] * rescale,
        gain_sums[1] * rescale,
    )


def solution(mesh):
    placed = (
        P("ctx", "tp", None),
        P("ctx", "tp", None),
        P("ctx", "tp", None),
        P(),
        P(),
        P(),
        P("ctx", "tp", None),
    )
    return jax.shard_map(
        on_device,
        mesh=mesh,
        in_specs=placed,
        out_specs=(P("ctx", "tp", None), P("ctx", "tp", None), P("ctx", "tp", None), P(), P()),
        check_vma=False,
    )
```
